32 devices in a mesh: space: 8 (over z, core), set: 4 (over y, x).
Axes of the slice: x: 2, y: 2, z: 4, core: 2. Of those that a mesh axis runs over, the one named last changes fastest.
Arguments:
- initial: float32 [8, 64, 256, 128], P('set', 'space'), may hold values from -6 to 6
- conductivity: float32 [64, 256, 128], P('space'), may hold values from 0.3 to 1
- weights: float32 [8, 64, 256, 128], P('set', 'space'), may hold values from -6 to 6
- setting_index: int32 [8], P('set'), may hold values from 0 to 63
- track: int32 [64, 4], replicated, may hold values from 0 to 255
- power: int32 [64, 4], replicated, may hold values from 0 to 3
Outputs:
- final_temperature: float32 [8, 64, 256, 128], P('set', 'space')
- conductivity_gradient: float32 [64, 256, 128], P('space', 'set')
The draws below stay inside these ranges and needn't reach their ends.
All inputs are finite; a program needn't handle non-finite values.
Results may differ from the reference program's by a relative error of at most 0.00002.
Values sent between devices are 32-bit elements; how exact they have to be, the bound alone decides.
No kernel may reach another device: no remote copies, remote signals or barrier semaphores. Data moves between devices by JAX's collectives and lax.ppermute only.
A program may use at most 128 MiB of HBM per device.

```python
import math
import jax
import jax.numpy as jnp
from jax import lax

NY = 256
NZ = 128
STEPS = 4
LASERS = 64
NPL = 64
SETTINGS = 8


def set_ends(array, rng, smallest, largest):
    longest = array.shape.index(max(array.shape))
    spots = []
    for shift in (0, 1):
        where = [jax.random.randint(jax.random.fold_in(rng, axis), (), 0, length) for axis, length in enumerate(array.shape)]
        where[longest] = (where[longest] + shift) % array.shape[longest]
        spots.append(tuple(where))
    return array.at[spots[0]].set(smallest).at[spots[1]].set(largest)


def strengthened(drawn, stream_key, source, target, shards_of, factor):
    def block_of(position):
        return (jnp.arange(drawn.shape[position]) // (drawn.shape[position] // shards_of)).reshape((-1,) + (1,) * (drawn.ndim - 1 - position))

    first = jax.random.permutation(stream_key, shards_of)[block_of(target)]
    other_side = (block_of(target) + shards_of // 2) % shards_of
    return jnp.where((block_of(source) == first) | (block_of(source) == other_side), factor * drawn, drawn)


def steps_of(own_key, shape, split, least, largest):
    level, own = 1.0, jax.random.fold_in(own_key, 6)
    for position, parts in split:
        steps = jnp.exp(jax.random.uniform(jax.random.fold_in(own, position), (parts,), jnp.float32, least / len(split), largest / len(split)))
        level = level * jnp.repeat(steps, shape[position] // parts).reshape([-1 if axis == position else 1 for axis in range(len(shape))])
    return level


def bell_draw(rng, extent, width, most, cuts=(), held_as=jnp.bfloat16):
    array = jax.random.normal(rng, extent, jnp.float32) * width
    if len(cuts) > 0:
        array = steps_of(rng, extent, cuts, -0.22, 0.18) * array
    return jnp.clip(array, min=-most, max=most).astype(held_as)


def noise_with(key, shape, width, reach, shards, heavy, dtype=jnp.bfloat16):
    array = width * jax.random.normal(key, shape, jnp.float32)
    if shards:
        array = array * steps_of(key, shape, shards, -0.22, 0.18)
    return jnp.clip(strengthened(array, jax.random.fold_in(key, 3), *heavy), -reach, reach).astype(dtype)


def setup_inputs(seed: int = 0) -> dict:
    keys = jax.random.split(jax.random.key(seed), 7)
    initial = bell_draw(keys[0], (SETTINGS, NPL, NY, NZ), 1.0, 6.0, ((0, 4), (1, 8)), jnp.float32)
    conductivity = jnp.clip(jnp.exp(math.log(1.0) - 1.2039728 * jax.random.uniform(keys[1], (NPL, NY, NZ), jnp.float32) ** steps_of(keys[1], (NPL, NY, NZ), ((0, 8),), -0.2, 0.2)), 0.3, 1.0)
    weights = noise_with(keys[2], (SETTINGS, NPL, NY, NZ), 1.0, 6.0, ((0, 4), (1, 8)), (0, 2, 4, 2.0), jnp.float32)
    setting_index = set_ends(jax.random.randint(keys[3], (SETTINGS,), 0, LASERS), jax.random.fold_in(keys[3], 1), 0, LASERS - 1).astype(jnp.int32)
    track = set_ends(jax.random.randint(keys[4], (LASERS, STEPS), 0, NY), jax.random.fold_in(keys[4], 1), 0, NY - 1).astype(jnp.int32)
    power = set_ends(jax.random.randint(keys[5], (LASERS, STEPS), 0, 4), jax.random.fold_in(keys[5], 1), 0, 3).astype(jnp.int32)
    return dict(initial=initial, conductivity=conductivity, weights=weights, setting_index=setting_index, track=track, power=power)


DT = 0.15

def conduct(thermal):
    return 1.0 / (1.0 + thermal * thermal)

def source_field(y_start, power_level):
    y_cells = jnp.arange(NY).astype(jnp.float32)
    z_cells = jnp.arange(NZ).astype(jnp.float32)
    offset = (y_cells - y_start) * 16.0 / NY
    prof_y = jnp.exp(-(offset * offset))
    prof_z = jnp.exp(-4.0 * z_cells / NZ)
    return 0.5 * (1.0 + power_level) * prof_y[:, None] * prof_z[None, :]

def advance(thermal, kappa, heat):
    coeffs = kappa * conduct(thermal)
    padded_temp = jnp.pad(thermal, 1)
    padded_coef = jnp.pad(coeffs, 1)
    slices = [(slice(2, None), slice(1, -1), slice(1, -1)), (slice(0, -2), slice(1, -1), slice(1, -1)), (slice(1, -1), slice(2, None), slice(1, -1)), (slice(1, -1), slice(0, -2), slice(1, -1)), (slice(1, -1), slice(1, -1), slice(2, None)), (slice(1, -1), slice(1, -1), slice(0, -2))]
    flux = jnp.zeros_like(thermal)
    for where in slices:
        flux = flux + 0.5 * (coeffs + padded_coef[where]) * (padded_temp[where] - thermal)
    return thermal + DT * (flux + heat[None])

def reference(initial, conductivity, weights, setting_index, track, power):

    def per_setting(carry, inputs):
        start_temp, weight_row, setting = inputs
        track_row = track[setting]
        power_row = power[setting]

        def forward(kappa):
            thermal = start_temp
            for index_step in range(STEPS):
                heat = source_field(track_row[index_step].astype(jnp.float32), power_row[index_step].astype(jnp.float32))
                thermal = advance(thermal, kappa, heat)
            return thermal
        final, pull_back = jax.vjp(forward, conductivity)
        pulled, = pull_back(weight_row)
        return (carry + pulled, final)
    gradient, finals = lax.scan(per_setting, jnp.zeros(conductivity.shape, jnp.float32), (initial, weights, setting_index))
    return (finals, gradient)
```

```python
import jax
import jax.numpy as jnp
from jax import lax
from jax.experimental import pallas as pl
from jax.experimental.pallas import tpu as pltpu
from jax.sharding import PartitionSpec as P

STEPS = 4
DT = 0.15
HALF = 0.5 * DT
DEPTH = 5
WDEPTH = 2
AHEAD = 14
F32 = jnp.float32


class Geometry:
    def __init__(self, shape):
        self.sets, self.planes, self.rows, self.lanes = shape
        self.tiles = self.rows // 8

    def padded(self, halo):
        return (self.sets, self.planes + 2 * halo, self.tiles + 2, 8, self.lanes)

    def single(self, halo):
        return (self.planes + 2 * halo, self.tiles, 8, self.lanes)

    def tile_row(self, t):
        return pl.ds(t, 8, stride=self.tiles)


def reciprocal(x):
    r = pltpu.reciprocal(x, approx=True)
    return r * (2.0 - x * r)


def loop(lo, hi, body):
    def step(i, _):
        body(i)
        return 0

    lax.fori_loop(lo, hi, step, 0)


class Lanes:
    def __init__(self, geo):
        self.count = geo.lanes
        lane = lax.broadcasted_iota(jnp.int32, (8, geo.lanes), 1)
        sub = lax.broadcasted_iota(jnp.int32, (8, geo.lanes), 0)
        self.inner = jnp.where(lane == geo.lanes - 1, 0.0, 1.0)
        self.ends = jnp.where((lane == geo.lanes - 1) | (lane == 0), 1.0, 0.0)
        self.first, self.last = sub == 0, sub == 7

    def next(self, x):
        return pltpu.roll(x, self.count - 1, 1)

    def previous(self, x):
        return pltpu.roll(x, 1, 1)

    def before(self, tile):
        return jnp.where(self.first, 0.0, pltpu.roll(tile, 1, 0))

    def after(self, tile):
        return jnp.where(self.last, 0.0, pltpu.roll(tile, 7, 0))

    def put(self, ref, s, d, t, tiles, value):
        ref[s, d, t + 1] = value
        if t == 0:
            ref[s, d, tiles + 1] = self.after(value)
        if t == tiles - 1:
            ref[s, d, 0] = self.before(value)


def staged(count, first, second, third):
    one, two = {}, {}
    for i in range(count + 2 * AHEAD):
        if i < count:
            one[i] = first(i)
        j = i - AHEAD
        if 0 <= j < count:
            two[j] = second(j, one.pop(j))
        j = i - 2 * AHEAD
        if 0 <= j < count:
            third(j, two.pop(j))


def weight_of(i, lo, edge):
    return HALF if edge is None else jnp.where(i < -lo, edge, HALF)


def forward(geo, off, lo, hi, u, a, heat, flux, edge, k, k_off, u_next, a_next, out=None):
    lanes = Lanes(geo)
    tiles = geo.tiles

    def start(t):
        for s in range(geo.sets):
            flux[0, s, t] = (a[s, lo + off, t + 1] + a[s, lo - 1 + off, t + 1]) * (
                u[s, lo + off, t + 1] - u[s, lo - 1 + off, t + 1]
            )

    lax.fori_loop(0, tiles, lambda t, c: (start(t), c)[1], 0, unroll=8)

    def plane(i):
        p = i + (lo + off)
        w = weight_of(i, lo, edge)
        items = [(s, t) for s in range(geo.sets) for t in range(tiles)]
        face = {}

        def first(m):
            s, t = items[m]
            return lanes.next(u[s, p, t + 1]), lanes.next(a[s, p, t + 1])

        def second(m, rolled):
            s, t = items[m]
            ur, ar = rolled
            f = (ar + a[s, p, t + 1]) * (ur - u[s, p, t + 1]) * lanes.inner
            return f, lanes.previous(f)

        def third(m, z):
            s, t = items[m]
            uc, ac = u[s, p, t + 1], a[s, p, t + 1]
            if t == 0:
                face[s] = (ac + a[s, p, 0]) * (uc - u[s, p, 0])
            fy = (a[s, p, t + 2] + ac) * (u[s, p, t + 2] - uc)
            fx = (a[s, p + 1, t + 1] + ac) * (u[s, p + 1, t + 1] - uc)
            total = (fx - flux[0, s, t]) + (fy - face[s]) + (z[0] - z[1]) - (ac * uc) * lanes.ends
            face[s] = fy
            flux[0, s, t] = fx
            new = uc + w * (total + heat[s, t])
            if out is not None:
                out(s, i + lo, t, new)
            else:
                lanes.put(u_next, s, p - 1, t, tiles, new)
                lanes.put(a_next, s, p - 1, t, tiles, k[i + (lo + k_off), t] * reciprocal(1.0 + new * new))

        staged(len(items), first, second, third)

    loop(0, hi - lo, plane)


def backward(geo, off, lo, hi, u, a, rk, lam, lam_off, lam_next, next_off, grad, flux, edge):
    lanes = Lanes(geo)
    tiles = geo.tiles
    last = lam_next is None

    def start(t):
        for s in range(geo.sets):
            dl = lam[s, lo + lam_off, t + 1] - lam[s, lo - 1 + lam_off, t + 1]
            flux[0, s, t] = (u[s, lo + off, t + 1] - u[s, lo - 1 + off, t + 1]) * dl
            if not last:
                flux[1, s, t] = (a[s, lo + off, t + 1] + a[s, lo - 1 + off, t + 1]) * dl

    lax.fori_loop(0, tiles, lambda t, c: (start(t), c)[1], 0, unroll=8)

    def plane(i):
        p, q, r = i + (lo + off), i + (lo + lam_off), i + (lo + 1)
        w = weight_of(i, lo, edge)
        items = [(s, t) for t in range(tiles) for s in range(geo.sets)]
        face, parts = {}, {}

        def first(m):
            s, t = items[m]
            rolled = lanes.next(u[s, p, t + 1]), lanes.next(lam[s, q, t + 1])
            return rolled if last else rolled + (lanes.next(a[s, p, t + 1]),)

        def second(m, rolled):
            s, t = items[m]
            dl = (rolled[1] - lam[s, q, t + 1]) * lanes.inner
            e = (rolled[0] - u[s, p, t + 1]) * dl
            if last:
                return e, lanes.previous(e)
            g = (rolled[2] + a[s, p, t + 1]) * dl
            return e, lanes.previous(e), g, lanes.previous(g)

        def third(m, z):
            s, t = items[m]
            uc, ac, lc = u[s, p, t + 1], a[s, p, t + 1], lam[s, q, t + 1]
            if t == 0:
                dl = lc - lam[s, q, 0]
                face[s] = (uc - u[s, p, 0]) * dl, (ac + a[s, p, 0]) * dl
            dl = lam[s, q, t + 2] - lc
            ey, gy = (u[s, p, t + 2] - uc) * dl, (a[s, p, t + 2] + ac) * dl
            dl = lam[s, q + 1, t + 1] - lc
            ex, gx = (u[s, p + 1, t + 1] - uc) * dl, (a[s, p + 1, t + 1] + ac) * dl
            le = lc * lanes.ends
            e = (ex + flux[0, s, t]) + (ey + face[s][0]) + (z[0] + z[1]) + uc * le
            flux[0, s, t] = ex
            b = e * (ac * rk[r, t])
            parts[t] = parts[t] + b if s else b
            if s == geo.sets - 1:
                grad[r, t] += parts.pop(t)
            if not last:
                g = (gx - flux[1, s, t]) + (gy - face[s][1]) + (z[2] - z[3]) - ac * le
                flux[1, s, t] = gx
                b = b * (ac * uc)
                lanes.put(lam_next, s, i + (lo + next_off), t, tiles, lc + w * (g + (b + b)))
            face[s] = ey, gy

        staged(len(items), first, second, third)

    loop(0, hi - lo, plane)


def place():
    me = lax.axis_index("space")
    joined = jnp.where((me == 0) | (me == lax.axis_size("space") - 1), 0, 1)
    return lax.rem(me, 2), joined


def flipped(geo, odd, d):
    return jnp.where(odd == 1, geo.planes - 1 - d, d)


def cut_kernel(geo, refs):
    initial, cond, weights, uo, ko, wo, ui, ki, wi, sems = refs
    odd, _ = place()
    copies = []
    for outer, u, k, w in ((True, uo, ko, wo), (False, ui, ki, wi)):
        def begin(depth):
            return jnp.where((odd == 1) == outer, geo.planes - depth, 0)

        for src, dst in (
            (initial.at[:, pl.ds(begin(DEPTH), DEPTH)], u),
            (cond.at[pl.ds(begin(DEPTH), DEPTH)], k),
            (weights.at[:, pl.ds(begin(WDEPTH), WDEPTH)], w),
        ):
            copies.append(pltpu.make_async_copy(src, dst, sems.at[len(copies)]))
    for c in copies:
        c.start()
    for c in copies:
        c.wait()


STATE = ("u0", "a0", "u1", "a1", "u2", "a2", "u3", "a3", "k", "rk", "lam", "grad", "heat")


def state_shapes(geo):
    shapes = []
    for n in range(STEPS):
        shapes += [geo.padded(DEPTH - n)] * 2
    shapes += [geo.single(DEPTH), geo.single(1), geo.padded(WDEPTH), geo.single(1)]
    return shapes + [(STEPS, geo.sets, geo.tiles, 8, geo.lanes)]


def unpack_plane(geo, lanes, p, value, cond, u0, a0, k):
    for t in range(geo.tiles):
        kap = cond(t)
        k[p, t] = kap
        for s in range(geo.sets):
            val = value(s, t)
            lanes.put(u0, s, p, t, geo.tiles, val)
            lanes.put(a0, s, p, t, geo.tiles, kap * reciprocal(1.0 + val * val))


def first_kernel(geo, refs):
    (initial, cond, weights, index_ref, track_ref, power_ref, u0, a0, u1, a1, u2, a2, u3, a3, k, rk, l4, grad, heat) = refs[:19]
    raw_u, raw_k, raw_w, flux, sems = refs[19:]
    odd, _ = place()
    top = geo.planes
    lanes = Lanes(geo)

    def copies(d):
        p = flipped(geo, odd, d)
        return (
            pltpu.make_async_copy(initial.at[:, p], raw_u.at[:, d], sems.at[0, d]),
            pltpu.make_async_copy(cond.at[p], raw_k.at[d], sems.at[1, d]),
            pltpu.make_async_copy(weights.at[:, p], raw_w.at[:, d], sems.at[2, d]),
        )

    def begin(d):
        for c in copies(d):
            c.start()

    loop(0, top, begin)
    z = lax.broadcasted_iota(jnp.int32, (8, geo.lanes), 1).astype(F32)
    prof_z = jnp.exp(-4.0 * z / geo.lanes)
    sub = lax.broadcasted_iota(jnp.int32, (8, geo.lanes), 0) * geo.tiles

    def warm(i):
        n, s = i // geo.sets, lax.rem(i, geo.sets)
        row = index_ref[s]
        y0 = track_ref[row, n]
        amp = (1.0 + power_ref[row, n].astype(F32)) * prof_z
        for t in range(geo.tiles):
            offset = (sub + (t - y0)).astype(F32) * (16.0 / geo.rows)
            heat[n, s, t] = amp * jnp.exp(-(offset * offset))

    loop(0, STEPS * geo.sets, warm)

    def clear(d):
        grad[d] = jnp.zeros((geo.tiles, 8, geo.lanes), F32)

    loop(0, top + 2, clear)

    def load(d):
        for c in copies(d):
            c.wait()
        unpack_plane(
            geo, lanes, d + DEPTH, lambda s, t: raw_u[s, d, geo.tile_row(t), :], lambda t: raw_k[d, geo.tile_row(t), :], u0, a0, k
        )
        for t in range(geo.tiles):
            rk[d + 1, t] = reciprocal(k[d + DEPTH, t])
            for s in range(geo.sets):
                lanes.put(l4, s, d + WDEPTH, t, geo.tiles, raw_w[s, d, geo.tile_row(t), :])

    loop(0, top, load)
    us, as_ = (u0, u1, u2, u3), (a0, a1, a2, a3)
    for n in range(STEPS - 1):
        forward(
            geo, DEPTH - n, n + 1, top - n - 1, us[n], as_[n], heat.at[n], flux, None, k, DEPTH, us[n + 1], as_[n + 1]
        )


def unpack_halo(geo, odd, u_src, k_src, w_src, u0, a0, k, rk, lam, outer):
    lanes = Lanes(geo)

    def local(j, depth):
        if outer:
            return jnp.where(odd == 1, depth - 1 - j, j)
        return jnp.where(odd == 1, depth - 1 - j, j) + (geo.planes + depth)

    def planes(j):
        unpack_plane(
            geo, lanes, local(j, DEPTH), lambda s, t: u_src[s, j, geo.tile_row(t), :],
            lambda t: k_src[j, geo.tile_row(t), :], u0, a0, k,
        )

    loop(0, DEPTH, planes)

    def more(j):
        for s in range(geo.sets):
            for t in range(geo.tiles):
                lanes.put(lam, s, local(j, WDEPTH), t, geo.tiles, w_src[s, j, geo.tile_row(t), :])

    loop(0, WDEPTH, more)
    d = -1 if outer else geo.planes
    for t in range(geo.tiles):
        rk[d + 1, t] = reciprocal(k[d + DEPTH, t])


def second_kernel(geo, refs):
    (ui, ki, wi) = refs[:3]
    (u0, a0, u1, a1, u2, a2, u3, a3, k, rk, lam, grad, heat, l3, send) = refs[16:31]
    flux = refs[31]
    odd, _ = place()
    top = geo.planes
    unpack_halo(geo, odd, ui, ki, wi, u0, a0, k, rk, lam, False)
    us, as_ = (u0, u1, u2, u3), (a0, a1, a2, a3)
    for n in range(STEPS - 1):
        forward(
            geo, DEPTH - n, top - n - 1, top + DEPTH - 1 - n, us[n], as_[n], heat.at[n], flux, None, k, DEPTH,
            us[n + 1], as_[n + 1],
        )
    backward(geo, 2, top - 4, top + 1, u3, a3, rk, lam, WDEPTH, l3, 1, grad, flux, None)
    backward(geo, 3, top - 3, top, u2, a2, rk, l3, 1, lam, WDEPTH, grad, flux, None)
    for s in range(geo.sets):
        for j in range(WDEPTH):
            send[s, j] = lam[s, top - 1 - j + WDEPTH]


def third_kernel(geo, refs):
    (uo, ko, wo) = refs[:3]
    (u0, a0, u1, a1, u2, a2, u3, a3, k, rk, lam, grad, l3, send) = refs[17:31]
    heat = refs[15]
    flux = refs[31]
    odd, joined = place()
    edge = HALF * joined.astype(F32)

    @pl.when(joined == 0)
    def _():
        zero = jnp.zeros((geo.tiles + 2, 8, geo.lanes), F32)
        def body(j):
            k[j] = zero[: geo.tiles]
            for s in range(geo.sets):
                u0[s, j] = zero
                a0[s, j] = zero

        loop(0, DEPTH, body)
        for s in range(geo.sets):
            for j in range(WDEPTH):
                lam[s, j] = zero
        rk[0] = zero[: geo.tiles]

    @pl.when(joined == 1)
    def _():
        unpack_halo(geo, odd, uo, ko, wo, u0, a0, k, rk, lam, True)

    us, as_ = (u0, u1, u2, u3), (a0, a1, a2, a3)
    for n in range(STEPS - 1):
        forward(
            geo, DEPTH - n, n + 1 - DEPTH, n + 1, us[n], as_[n], heat.at[n], flux, edge, k, DEPTH, us[n + 1], as_[n + 1]
        )
    backward(geo, 2, -1, 3, u3, a3, rk, lam, WDEPTH, l3, 1, grad, flux, edge)
    backward(geo, 3, 0, 2, u2, a2, rk, l3, 1, lam, WDEPTH, grad, flux, edge)
    for s in range(geo.sets):
        for j in range(WDEPTH):
            send[s, j] = lam[s, j + WDEPTH]


def fourth_kernel(geo, refs):
    (u0, a0, u1, a1, u2, a2, u3, a3, rk, heat, received) = refs[:11]
    (final, lam, l3, grad) = refs[14:18]
    flux, raw, sems = refs[18:]
    odd, _ = place()
    top = geo.planes

    def put(s, d, t, value):
        raw[s, d, geo.tile_row(t), :] = value

    forward(geo, 2, 0, top, u3, a3, heat.at[3], flux, None, None, 0, None, None, out=put)

    def copy(d):
        return pltpu.make_async_copy(raw.at[:, d], final.at[:, flipped(geo, odd, d)], sems.at[d])

    loop(0, top, lambda d: copy(d).start())
    for s in range(geo.sets):
        for j in range(WDEPTH):
            lam[s, top + WDEPTH + j] = received[s, j]
    backward(geo, 2, 3, top - 4, u3, a3, rk, lam, WDEPTH, l3, 1, grad, flux, None)
    backward(geo, 3, 2, top - 3, u2, a2, rk, l3, 1, lam, WDEPTH, grad, flux, None)
    backward(geo, 4, 1, top + 1, u1, a1, rk, lam, WDEPTH, l3, 1, grad, flux, None)
    backward(geo, 5, 2, top, u0, a0, rk, l3, 1, None, 0, grad, flux, None)
    loop(0, top, lambda d: copy(d).wait())


def fifth_kernel(geo, ways, refs):
    (u0, a0, u1, a1, rk, received) = refs[:6]
    (lam, l3, grad) = refs[9:12]
    outs = refs[12 : 12 + ways]
    flux, flat = refs[12 + ways :]
    _, joined = place()
    edge = HALF * joined.astype(F32)
    for s in range(geo.sets):
        for j in range(WDEPTH):
            lam[s, WDEPTH - 1 - j] = jnp.where(joined == 1, received[s, j], 0.0)
    backward(geo, 4, -1, 1, u1, a1, rk, lam, WDEPTH, l3, 1, grad, flux, edge)
    backward(geo, 5, 0, 2, u0, a0, rk, l3, 1, None, 0, grad, flux, None)
    me = lax.axis_index("set")
    part = geo.rows // ways

    def spread(d):
        for t in range(geo.tiles):
            flat[geo.tile_row(t), :] = grad[d + 1, t] * (-HALF)
        for way in range(ways):
            outs[way][d] = flat[pl.ds(pl.multiple_of((me ^ way) * part, part), part), :]

    loop(0, geo.planes, spread)


def sum_kernel(geo, refs):
    odd, _ = place()

    def body(d):
        total = refs[0][d]
        for ref in refs[1:-1]:
            total += ref[d]
        refs[-1][flipped(geo, odd, d)] = total

    loop(0, geo.planes, body)


VMEM = pl.BlockSpec(memory_space=pltpu.VMEM)
SMEM = pl.BlockSpec(memory_space=pltpu.SMEM)
HBM = pl.BlockSpec(memory_space=pltpu.HBM)


def pinned(shape):
    return pltpu.VMEM(shape, F32)


def plain(shape):
    return jax.ShapeDtypeStruct(shape, F32)


def call(body, name, ins, in_specs, outs, out_specs=None, aliases=None, scratch=(), mib=4):
    return pl.pallas_call(
        lambda *refs: body(refs),
        name=name,
        out_shape=tuple(outs),
        in_specs=list(in_specs),
        out_specs=tuple(out_specs or [VMEM] * len(outs)),
        scratch_shapes=list(scratch),
        input_output_aliases=aliases or {},
        compiler_params=pltpu.CompilerParams(vmem_limit_bytes=mib * 1024 * 1024),
    )(*ins)


def keep(x):
    return pltpu.with_memory_space_constraint(x, pltpu.VMEM)


def outside(x):
    return pltpu.with_memory_space_constraint(x, pltpu.HBM)


def local(initial, conductivity, weights, setting_index, track, power):
    geo = Geometry(initial.shape)
    top = geo.planes
    spaces, ways = lax.axis_size("space"), lax.axis_size("set")

    both = ("space", "set")
    pairs = [(i, i + 1) for i in range(1, spaces - 1, 2)]
    outer = [(a * ways + c, b * ways + c) for i, j in pairs for a, b in ((i, j), (j, i)) for c in range(ways)]
    outer += [(e * ways + c, e * ways + (c ^ 1)) for e in (0, spaces - 1) for c in range(ways)]
    inner = [(i, i ^ 1) for i in range(spaces)]

    cut_u = (geo.sets, DEPTH, geo.rows, geo.lanes)
    cut_k = (DEPTH, geo.rows, geo.lanes)
    cut_w = (geo.sets, WDEPTH, geo.rows, geo.lanes)
    cuts = call(
        lambda refs: cut_kernel(geo, refs), "cut", tuple(outside(x) for x in (initial, conductivity, weights)), [HBM] * 3,
        [pinned(x) for x in (cut_u, cut_k, cut_w) * 2], scratch=[pltpu.SemaphoreType.DMA((6,))], mib=6,
    )
    uo, ko, wo = (lax.ppermute(x, both, outer) for x in cuts[:3])
    ui, ki, wi = (lax.ppermute(x, "space", inner) for x in cuts[3:])

    flux = pltpu.VMEM((2, geo.sets, geo.tiles, 8, geo.lanes), F32)
    states = [pinned(x) for x in state_shapes(geo)]
    state = call(
        lambda refs: first_kernel(geo, refs), "first",
        tuple(outside(x) for x in (initial, conductivity, weights)) + (setting_index, track, power),
        [HBM] * 3 + [SMEM] * 3, states,
        scratch=[
            pltpu.VMEM(initial.shape, F32), pltpu.VMEM(conductivity.shape, F32), pltpu.VMEM(weights.shape, F32),
            flux, pltpu.SemaphoreType.DMA((3, top)),
        ],
        mib=8,
    )
    l3_shape = pinned(geo.padded(1))
    send = pinned((geo.sets, WDEPTH, geo.tiles + 2, 8, geo.lanes))
    result = call(
        lambda refs: second_kernel(geo, refs), "second",
        tuple(keep(x) for x in (ui, ki, wi) + tuple(state)), [VMEM] * 16, states + [l3_shape, send],
        aliases={3 + i: i for i in range(13)}, scratch=[flux],
    )
    state, l3, send_i = result[:12], result[13], result[14]
    heat = result[12]
    from_inner = lax.ppermute(send_i, "space", inner)
    result = call(
        lambda refs: third_kernel(geo, refs), "third",
        tuple(keep(x) for x in (uo, ko, wo) + tuple(state) + (heat, l3)), [VMEM] * 17, states[:12] + [l3_shape, send],
        aliases={**{3 + i: i for i in range(12)}, 16: 12}, scratch=[flux],
    )
    u0, a0, u1, a1, u2, a2, u3, a3, k, rk, lam, grad, l3, send_o = result
    from_outer = lax.ppermute(send_o, both, outer)
    final, lam, l3, grad = call(
        lambda refs: fourth_kernel(geo, refs), "fourth",
        tuple(keep(x) for x in (u0, a0, u1, a1, u2, a2, u3, a3, rk, heat, from_inner, lam, l3, grad)), [VMEM] * 14,
        [plain(initial.shape), states[10], l3_shape, states[11]], out_specs=[HBM] + [VMEM] * 3,
        aliases={11: 1, 12: 2, 13: 3},
        scratch=[flux, pltpu.VMEM(initial.shape, F32), pltpu.SemaphoreType.DMA((top,))], mib=4,
    )
    part = (top, geo.rows // ways, geo.lanes)
    result = call(
        lambda refs: fifth_kernel(geo, ways, refs), "fifth",
        tuple(keep(x) for x in (u0, a0, u1, a1, rk, from_outer, lam, l3, grad)), [VMEM] * 9,
        [states[10], l3_shape, states[11]] + [pinned(part)] * ways, aliases={6: 0, 7: 1, 8: 2},
        scratch=[flux, pltpu.VMEM((geo.rows, geo.lanes), F32)],
    )
    parts = result[3:]
    arrived = [parts[0]]
    for way in range(1, ways):
        arrived.append(lax.ppermute(parts[way], "set", [(i, i ^ way) for i in range(ways)]))
    (owned,) = call(
        lambda refs: sum_kernel(geo, refs), "total", tuple(keep(x) for x in arrived), [VMEM] * ways, [plain(part)]
    )
    return (final, owned)


def solution(mesh):
    in_specs = (
        P("set", "space", None, None),
        P("space", None, None),
        P("set", "space", None, None),
        P("set"),
        P(),
        P(),
    )
    out_specs = (P("set", "space", None, None), P("space", "set", None))
    return jax.shard_map(local, mesh=mesh, in_specs=in_specs, out_specs=out_specs, check_vma=False)
```
